128 devices in a mesh: site: 4 (over x), row: 4 (over y_hi, core), col: 8 (over y_lo, z).
Axes of the slice: x: 4, y: 4 (y_hi: 2, y_lo: 2; y = y_hi * 2 + y_lo), z: 4, core: 2. Of those that a mesh axis runs over, the one named last changes fastest.
Arguments:
- cores_x: bfloat16 [4, 1536, 8, 1536], P('site', 'col', None, 'row'), may hold values from -0.09375 to 0.09375
- cores_y: bfloat16 [4, 1536, 8, 1536], P('site', 'col', None, 'row'), may hold values from -0.09375 to 0.09375
- left_env: bfloat16 [1536, 1536], P('col', 'row'), may hold values from -6 to 6
- right_env: bfloat16 [1536, 1536], P('col', 'row'), may hold values from -0.15625 to 0.15625
Outputs:
- gradient: float32 [4, 1536, 8, 1536], P('site', 'col', None, 'row')
The draws below stay inside these ranges and needn't reach their ends.
All inputs are finite; a program needn't handle non-finite values.
Results may differ from the reference program's by a relative error of at most 0.025.
Values may be sent and summed in bfloat16 or wider, within the bound.
No kernel may reach another device: no remote copies, remote signals or barrier semaphores. Data moves between devices by JAX's collectives and lax.ppermute only.
A program may use at most 128 MiB of HBM per device.

```python
import jax
import jax.numpy as jnp
from jax import lax

BOND = 1536
MODE = 8
CORES = 4


def steps_of(stream_key, shape, pieces, smallest, high):
    level = 1.0
    for position, parts in pieces:
        heights = jax.random.uniform(jax.random.fold_in(jax.random.fold_in(stream_key, 6), position), (parts,), jnp.float32, smallest / len(pieces), high / len(pieces))
        level = level * jnp.repeat(jnp.exp(heights), shape[position] // parts).reshape((-1,) + (1,) * (len(shape) - 1 - position))
    return level


def normal_values(rng, shape, deviation, most, pieces=(), dtype=jnp.bfloat16):
    result = deviation * jax.random.normal(rng, shape, jnp.float32)
    if pieces:
        result = result * steps_of(rng, shape, pieces, -0.22, 0.18)
    return jnp.clip(result, -most, most).astype(dtype)


def setup_inputs(seed: int = 0) -> dict:
    splits = jax.random.split(jax.random.key(seed), 5)
    return {
        "cores_x": normal_values(splits[0], (CORES, BOND, MODE, BOND), (3 * BOND) ** -0.5, 0.09375, ((0, 4), (1, 8), (3, 4))),
        "cores_y": normal_values(splits[1], (CORES, BOND, MODE, BOND), (3 * BOND) ** -0.5, 0.09375, ((0, 4), (1, 8), (3, 4))),
        "left_env": normal_values(splits[2], (BOND, BOND), 1.0, 6.0, ((0, 8), (1, 4))),
        "right_env": normal_values(splits[3], (BOND, BOND), BOND ** -0.5, 0.15625, ((0, 8), (1, 4))),
    }


def reference(cores_x, cores_y, left_env, right_env):
    left_list = []
    left_now = left_env
    mixed_list = []
    for index in range(CORES):
        left_list.append(left_now)
        y_flat = cores_y[index].reshape(BOND, MODE * BOND)
        mixed_core = jnp.dot(left_now, y_flat, preferred_element_type=jnp.float32).astype(jnp.bfloat16)
        mixed_core = mixed_core.reshape(BOND * MODE, BOND)
        mixed_list.append(mixed_core)
        if index < CORES - 1:
            x_flat = cores_x[index].reshape(BOND * MODE, BOND)
            summed = lax.dot_general(x_flat, mixed_core, (((0,), (0,)), ((), ())), preferred_element_type=jnp.float32)
            left_now = summed.astype(jnp.bfloat16)
    right_list = [None] * CORES
    right_now = right_env.T
    for index in range(CORES - 1, -1, -1):
        right_list[index] = right_now
        if index > 0:
            x_flat = cores_x[index].reshape(BOND * MODE, BOND)
            image_rows = lax.dot_general(x_flat, right_now, (((1,), (1,)), ((), ())), preferred_element_type=jnp.float32)
            image_rows = image_rows.astype(jnp.bfloat16).reshape(BOND, MODE * BOND)
            y_flat = cores_y[index].reshape(BOND, MODE * BOND)
            summed = lax.dot_general(y_flat, image_rows, (((1,), (1,)), ((), ())), preferred_element_type=jnp.float32)
            right_now = summed.astype(jnp.bfloat16)
    results = []
    for index in range(CORES):
        grad_core = jnp.dot(mixed_list[index], right_list[index], preferred_element_type=jnp.float32)
        results.append(grad_core.reshape(BOND, MODE, BOND))
    return jnp.stack(results, axis=0)
```

```python
import jax
import jax.numpy as jnp
from jax import lax
from jax.experimental import pallas as pl
from jax.experimental.pallas import tpu as pltpu
from jax.sharding import Mesh, PartitionSpec as P


AXES = ("x", "yh", "co", "yl", "z")
BF = jnp.bfloat16
F32 = jnp.float32


def moved(value, where):
    pairs = []
    for x in range(4):
        for yh in range(2):
            for co in range(2):
                for yl in range(2):
                    for z in range(4):
                        to = where(x, 2 * yh + yl, co, z)
                        if to is None:
                            continue
                        tx, ty, tc, tz = to
                        ty, tz = ty % 4, tz % 4
                        here = (((x * 2 + yh) * 2 + co) * 2 + yl) * 4 + z
                        there = (((tx * 2 + ty // 2) * 2 + tc) * 2 + ty % 2) * 4 + tz
                        pairs.append((here, there))
    return lax.ppermute(value, AXES, pairs)


def partner(x, y, co, z):
    return x, y, 1 - co, z


def placed(shape, pieces, offsets):
    rank = len(shape)
    table = jnp.stack([jnp.asarray(o, jnp.int32) for off in offsets for o in off])
    count = len(pieces)

    def kernel(table_ref, *refs):
        ins, out, sems = refs[:count], refs[count], refs[count + 1]
        copies = []
        for n in range(count):
            index = []
            for d in range(rank):
                size = pieces[n].shape[d]
                if size == shape[d]:
                    index.append(slice(None))
                else:
                    start = table_ref[n * rank + d]
                    if d >= rank - 2:
                        start = pl.multiple_of(start, 192 if d == rank - 2 else 384)
                    index.append(pl.ds(start, size))
            copies.append(pltpu.make_async_copy(ins[n], out.at[tuple(index)], sems.at[n]))
        for copy in copies:
            copy.start()
        for copy in copies:
            copy.wait()

    return pl.pallas_call(
        kernel,
        out_shape=jax.ShapeDtypeStruct(shape, pieces[0].dtype),
        in_specs=[pl.BlockSpec(memory_space=pltpu.SMEM)]
        + [pl.BlockSpec(memory_space=pl.ANY)] * count,
        out_specs=pl.BlockSpec(memory_space=pl.ANY),
        scratch_shapes=[pltpu.SemaphoreType.DMA((count,))],
    )(table, *pieces)


def dot(a, b, dims):
    return lax.dot_general(a, b, (dims, ((), ())), preferred_element_type=F32)


def on_device(cores_x, cores_y, left_env, right_env):
    site = lax.axis_index("x")
    yh, yl = lax.axis_index("yh"), lax.axis_index("yl")
    co, z = lax.axis_index("co"), lax.axis_index("z")
    y = 2 * yh + yl

    x_modes = jnp.transpose(cores_x[0], (1, 0, 2))
    y_modes = jnp.transpose(cores_y[0], (1, 0, 2))

    def half(modes, which):
        return lax.dynamic_slice_in_dim(modes, which * 4, 4, axis=0)

    piece = moved(
        jnp.where(site == 0, left_env, right_env),
        lambda x, y, co, z: (x, (y // 2) * 2 + co, y % 2, z),
    )

    y_a = moved(half(y_modes, yl), lambda x, y, co, z: (x, (y // 2) * 2 + co, y % 2, z))
    y_b = moved(half(y_modes, 1 - yl), lambda x, y, co, z: (x, (y // 2) * 2 + co, 1 - y % 2, z))
    y_a, y_b = y_a[:, None, None], y_b[:, None, None]
    y_piece = placed((4, 2, 1, 192, 384), [y_a, y_b], [(0, co, 0, 0, 0), (0, 1 - co, 0, 0, 0)])
    y_parts = [y_piece] + [
        moved(y_piece, lambda x, y, co, z, s=s: (x, y, co, z - s)) for s in (1, 3, 2)
    ]
    y_full = placed(
        (4, 2, 4, 192, 384), y_parts, [(0, 0, (z + s) % 4, 0, 0) for s in (0, 1, 3, 2)]
    ).reshape(4, 1536, 384)

    x_own = half(x_modes, co)
    x_other = moved(half(x_modes, 1 - co), partner)
    x_piece = placed((4, 192, 768), [x_own, x_other], [(0, 0, co * 384), (0, 0, (1 - co) * 384)])
    x_parts = [x_piece] + [
        moved(x_piece, lambda x, y, co, z, s=s: (x, y - s, co, z)) for s in (1, 3, 2)
    ]
    x_full = placed(
        (4, 384, 1536),
        x_parts,
        [(0, ((y + s) % 2) * 192, (((y + s) % 4) // 2) * 768) for s in (0, 1, 3, 2)],
    ).reshape(1536, 1536)

    def gathered(piece, t):
        def where(s):
            def to(x, y, co, z):
                if x == t:
                    return x, y - s, co, z
                if x == 3 - t:
                    return x, y, co, z - s
                return None
            return to
        parts = [piece] + [moved(piece, where(s)) for s in (1, 3, 2)]
        own = jnp.stack(parts)
        other = moved(
            own, lambda x, y, co, z: (x, y, 1 - co, z) if x in (t, 3 - t) else None
        )
        return own, other

    def left_of(own, other):
        pieces, offsets = [], []
        for c, stack in ((co, own), (1 - co, other)):
            for n, s in enumerate((0, 1, 3, 2)):
                pieces.append(stack[n])
                offsets.append((c * 192, ((y + s) % 4) * 384))
        return placed((384, 1536), pieces, offsets)

    def right_of(own, other):
        pieces, offsets = [], []
        for c, stack in ((co, own), (1 - co, other)):
            for n, s in enumerate((0, 1, 3, 2)):
                pieces.append(stack[n])
                offsets.append((c * 768 + ((z + s) % 4) * 192, 0))
        return placed((1536, 384), pieces, offsets)

    def mixed_of(left):
        return jnp.concatenate(
            [dot(left, y_full[i], ((1,), (0,))).astype(BF) for i in range(4)], axis=0
        )

    def left_step(own, other, mixed, right):
        mixed = mixed_of(left_of(own, other))
        out = dot(x_full, mixed, ((0,), (0,))).astype(BF)
        return out.reshape(2, 4, 192, 384).transpose(1, 0, 2, 3), mixed, right

    def right_step(own, other, mixed, right):
        right = right_of(own, other)
        image = dot(x_full, right, ((1,), (0,))).astype(BF)
        out = 0.0
        for i in range(4):
            out = out + dot(image[i * 384:(i + 1) * 384], y_full[i], ((1,), (1,)))
        out = out.astype(BF)
        return out.reshape(2, 192, 4, 384).transpose(2, 0, 1, 3), mixed, right

    def idle_step(own, other, mixed, right):
        return jnp.zeros((4, 2, 192, 384), BF), mixed, right

    mixed = jnp.zeros((1536, 384), BF)
    right = jnp.zeros((1536, 384), BF)
    for t in range(3):
        own, other = gathered(piece, t)
        role = jnp.where(site == t, 1, jnp.where(site == 3 - t, 2, 0))
        parts, mixed, right = lax.switch(
            role, [idle_step, left_step, right_step], own, other, mixed, right
        )
        active = (t, 3 - t)
        mine = lax.dynamic_index_in_dim(parts, co, 1, keepdims=False)
        theirs = lax.dynamic_index_in_dim(parts, 1 - co, 1, keepdims=False)
        theirs = moved(
            theirs, lambda x, y, co, z: (x, y, 1 - co, z) if x in active else None
        )
        both = (mine.astype(F32) + theirs.astype(F32)).astype(BF)
        me = jnp.where(site == t, z, y)

        def to(s):
            def where(x, y, co, z):
                if x == t:
                    return x, y, co, z + s
                if x == 3 - t:
                    return x, y + s, co, z
                return None
            return where

        def block(s):
            return lax.dynamic_index_in_dim(both, (me + s) % 4, 0, keepdims=False)

        total = block(0).astype(F32)
        for s in (1, 3, 2):
            total = total + moved(block(s), to(s)).astype(F32)

        def hop(x, y, co, z):
            if x == t:
                return x + 1, y, co, z
            if x == 3 - t:
                return x - 1, y, co, z
            return None

        piece = moved(total.astype(BF), hop)

    own, other = gathered(piece, 3)
    mixed, right = lax.switch(
        jnp.where(site == 3, 1, jnp.where(site == 0, 2, 0)),
        [
            lambda own, other, mixed, right: (mixed, right),
            lambda own, other, mixed, right: (mixed_of(left_of(own, other)), right),
            lambda own, other, mixed, right: (mixed, right_of(own, other)),
        ],
        own, other, mixed, right,
    )
    grad = dot(mixed, right, ((1,), (1,))).astype(BF).reshape(4, 2, 192, 4, 384)

    def grad_block(s, c):
        ty = (y + s) % 4
        q = (ty // 2) * 2 + (co + c) % 2
        out = lax.dynamic_slice(grad, (0, ty % 2, 0, q, 0), (4, 1, 192, 1, 384))
        return out.reshape(4, 192, 384)

    halves = []
    for c in (0, 1):
        total = 0.0
        for s in (1, 3, 2, 0):
            block = grad_block(s, c)
            if (s, c) != (0, 0):
                block = moved(
                    block, lambda x, y, co, z, s=s, c=c: (x, y + s, (co + c) % 2, z)
                )
            total = total + block.astype(F32)
        halves.append(total)
    first = jnp.where(co == 0, halves[0], halves[1])
    second = jnp.where(co == 0, halves[1], halves[0])
    whole = jnp.concatenate([first, second], axis=0)
    return jnp.transpose(whole, (1, 0, 2))[None]


def solution(mesh):
    fine = Mesh(mesh.devices.reshape(4, 2, 2, 2, 4), AXES)
    cores = P("x", ("yl", "z"), None, ("yh", "co"))
    env = P(("yl", "z"), ("yh", "co"))
    return jax.shard_map(
        on_device,
        mesh=fine,
        in_specs=(cores, cores, env, env),
        out_specs=cores,
        check_vma=False,
    )
```

```python
import jax
import jax.numpy as jnp
from jax import lax
from jax.experimental import pallas as pl
from jax.experimental.pallas import tpu as pltpu
from jax.sharding import Mesh, PartitionSpec as P


AXES = ("x", "yh", "co", "yl", "z")
BF = jnp.bfloat16
F32 = jnp.float32


def moved(value, where):
    pairs = []
    for x in range(4):
        for yh in range(2):
            for co in range(2):
                for yl in range(2):
                    for z in range(4):
                        to = where(x, 2 * yh + yl, co, z)
                        if to is None:
                            continue
                        tx, ty, tc, tz = to
                        ty, tz = ty % 4, tz % 4
                        here = (((x * 2 + yh) * 2 + co) * 2 + yl) * 4 + z
                        there = (((tx * 2 + ty // 2) * 2 + tc) * 2 + ty % 2) * 4 + tz
                        pairs.append((here, there))
    return lax.ppermute(value, AXES, pairs)


def index_of(x, y, co, z):
    return (((x * 2 + y // 2) * 2 + co) * 2 + y % 2) * 4 + z


def partner(x, y, co, z):
    return x, y, 1 - co, z


def placed(shape, pieces, offsets):
    rank = len(shape)
    table = jnp.stack([jnp.asarray(o, jnp.int32) for off in offsets for o in off])
    count = len(pieces)

    def kernel(table_ref, *refs):
        ins, out, sems = refs[:count], refs[count], refs[count + 1]
        copies = []
        for n in range(count):
            index = []
            for d in range(rank):
                size = pieces[n].shape[d]
                if size == shape[d]:
                    index.append(slice(None))
                else:
                    start = table_ref[n * rank + d]
                    if d >= rank - 2:
                        start = pl.multiple_of(start, 192 if d == rank - 2 else 384)
                    index.append(pl.ds(start, size))
            copies.append(pltpu.make_async_copy(ins[n], out.at[tuple(index)], sems.at[n]))
        for copy in copies:
            copy.start()
        for copy in copies:
            copy.wait()

    return pl.pallas_call(
        kernel,
        out_shape=jax.ShapeDtypeStruct(shape, pieces[0].dtype),
        in_specs=[pl.BlockSpec(memory_space=pltpu.SMEM)]
        + [pl.BlockSpec(memory_space=pl.ANY)] * count,
        out_specs=pl.BlockSpec(memory_space=pltpu.VMEM),
        scratch_shapes=[pltpu.SemaphoreType.DMA((count,))],
    )(table, *pieces)


def dot(a, b, dims):
    return lax.dot_general(a, b, (dims, ((), ())), preferred_element_type=F32)


def chain_step(scalars, own, other, x_full, y_full):
    def kernel(scalars_ref, own_ref, other_ref, x_ref, y_ref,
               theirs_ref, mine_ref, mixed_ref, right_ref, left_s, sum_l, sum_r):
        i = pl.program_id(0)
        role, co = scalars_ref[0], scalars_ref[1]
        halves = ((co, own_ref), (1 - co, other_ref))

        @pl.when(role == 1)
        def _():
            @pl.when(i == 0)
            def _():
                for h, ref in halves:
                    for j in range(4):
                        rows = pl.ds(pl.multiple_of(h * 192, 192), 192)
                        left_s[rows, j * 384:(j + 1) * 384] = ref[j]
                sum_l[...] = jnp.zeros_like(sum_l)

            mixed = jnp.dot(left_s[...], y_ref[0], preferred_element_type=F32).astype(BF)
            mixed_ref[0] = mixed
            sum_l[...] += dot(x_ref[0], mixed, ((0,), (0,)))

            @pl.when(i == 3)
            def _():
                for h, to in ((co, mine_ref), (1 - co, theirs_ref)):
                    for j in range(4):
                        rows = pl.ds(pl.multiple_of(h * 768 + j * 192, 192), 192)
                        to[j] = sum_l[rows, :].astype(to.dtype)

        @pl.when(role == 2)
        def _():
            @pl.when(i == 0)
            def _():
                for h, ref in halves:
                    for j in range(4):
                        rows = pl.ds(pl.multiple_of(h * 768 + j * 192, 192), 192)
                        right_ref[rows, :] = ref[j]
                sum_r[...] = jnp.zeros_like(sum_r)

            image = jnp.dot(x_ref[0], right_ref[...], preferred_element_type=F32).astype(BF)
            sum_r[...] += dot(image, y_ref[0], ((1,), (1,)))

            @pl.when(i == 3)
            def _():
                for h, to in ((co, mine_ref), (1 - co, theirs_ref)):
                    for j in range(4):
                        rows = pl.ds(pl.multiple_of(h * 192, 192), 192)
                        to[j] = sum_r[rows, j * 384:(j + 1) * 384].astype(to.dtype)

    whole = lambda *shape: pl.BlockSpec(shape, lambda i: (0,) * len(shape))
    per_mode = lambda *shape: pl.BlockSpec((1,) + shape, lambda i: (i, 0, 0))
    return pl.pallas_call(
        kernel,
        grid=(4,),
        out_shape=(
            jax.ShapeDtypeStruct((4, 192, 384), BF),
            jax.ShapeDtypeStruct((4, 192, 384), F32),
            jax.ShapeDtypeStruct((4, 384, 384), BF),
            jax.ShapeDtypeStruct((1536, 384), BF),
        ),
        in_specs=[
            pl.BlockSpec(memory_space=pltpu.SMEM),
            whole(4, 192, 384),
            whole(4, 192, 384),
            per_mode(384, 1536),
            per_mode(1536, 384),
        ],
        out_specs=(
            whole(4, 192, 384),
            whole(4, 192, 384),
            per_mode(384, 384),
            whole(1536, 384),
        ),
        scratch_shapes=[
            pltpu.VMEM((384, 1536), BF),
            pltpu.VMEM((1536, 384), F32),
            pltpu.VMEM((384, 1536), F32),
        ],
    )(scalars, own, other, x_full, y_full)


def on_device(cores_x, cores_y, left_env, right_env):
    site = lax.axis_index("x")
    yh, yl = lax.axis_index("yh"), lax.axis_index("yl")
    co, z = lax.axis_index("co"), lax.axis_index("z")
    y = 2 * yh + yl

    x_modes = jnp.transpose(cores_x[0], (1, 0, 2))
    y_modes = jnp.transpose(cores_y[0], (1, 0, 2))

    def half(modes, which):
        return lax.dynamic_slice_in_dim(modes, which * 4, 4, axis=0)

    piece = moved(
        jnp.where(site == 0, left_env, right_env),
        lambda x, y, co, z: (x, (y // 2) * 2 + co, y % 2, z),
    )

    def rings(t, left_along_y):
        groups = []
        for x in range(4):
            along_y = left_along_y != (x == 3 - t)
            for c in range(2):
                for other in range(4):
                    groups.append([
                        index_of(x, k, c, other) if along_y else index_of(x, other, c, k)
                        for k in range(4)
                    ])
        return groups

    def exchanged(value, groups):
        return lax.all_to_all(value, AXES, 0, 0, axis_index_groups=groups, tiled=True)

    def gathered(piece, t):
        own = exchanged(jnp.broadcast_to(piece, (4, 192, 384)), rings(t, True))
        other = moved(
            own, lambda x, y, co, z: (x, y, 1 - co, z) if x in (t, 3 - t) else None
        )
        return own, other

    y_a = moved(half(y_modes, yl), lambda x, y, co, z: (x, (y // 2) * 2 + co, y % 2, z))
    y_b = moved(half(y_modes, 1 - yl), lambda x, y, co, z: (x, (y // 2) * 2 + co, 1 - y % 2, z))
    y_a, y_b = y_a[:, None, None], y_b[:, None, None]
    y_piece = placed((4, 2, 1, 192, 384), [y_a, y_b], [(0, co, 0, 0, 0), (0, 1 - co, 0, 0, 0)])
    x_own = half(x_modes, co)
    x_other = moved(half(x_modes, 1 - co), partner)
    x_piece = placed((4, 192, 768), [x_own, x_other], [(0, 0, co * 384), (0, 0, (1 - co) * 384)])
    y_piece, x_piece, first = lax.optimization_barrier((y_piece, x_piece, gathered(piece, 0)))
    y_parts = [y_piece] + [
        moved(y_piece, lambda x, y, co, z, s=s: (x, y, co, z - s)) for s in (1, 3, 2)
    ]
    y_full = placed(
        (4, 2, 4, 192, 384), y_parts, [(0, 0, (z + s) % 4, 0, 0) for s in (0, 1, 3, 2)]
    ).reshape(4, 1536, 384)

    x_parts = [x_piece] + [
        moved(x_piece, lambda x, y, co, z, s=s: (x, y - s, co, z)) for s in (1, 3, 2)
    ]
    x_full = placed(
        (4, 384, 1536),
        x_parts,
        [(0, ((y + s) % 2) * 192, (((y + s) % 4) // 2) * 768) for s in (0, 1, 3, 2)],
    ).reshape(1536, 1536)

    x_full = x_full.reshape(4, 384, 1536)

    def stepped(t, own, other):
        role = jnp.where(site == t, 1, jnp.where(site == 3 - t, 2, 0))
        return chain_step(jnp.stack([role, co]).astype(jnp.int32), own, other, x_full, y_full)

    mixed, right = 0, 0
    for t in range(3):
        own, other = first if t == 0 else gathered(piece, t)
        theirs, mine, mixed_now, right_now = stepped(t, own, other)
        mixed = mixed_now if t == 0 else jnp.where(site == t, mixed_now, mixed)
        right = right_now if t == 0 else jnp.where(site == 3 - t, right_now, right)
        theirs = moved(
            theirs, lambda x, y, co, z: (x, y, 1 - co, z) if x in (t, 3 - t) else None
        )
        both = (mine + theirs.astype(F32)).astype(BF)
        both = exchanged(both, rings(t, False))
        total = jnp.sum(both.astype(F32), axis=0).astype(BF)

        def hop(x, y, co, z):
            if x == t:
                return x + 1, y, co, z
            if x == 3 - t:
                return x - 1, y, co, z
            return None

        piece = moved(total, hop)

    own, other = gathered(piece, 3)
    _, _, mixed_now, right_now = stepped(3, own, other)
    mixed = jnp.where(site == 3, mixed_now, mixed)
    right = jnp.where(site == 0, right_now, right)
    mixed = mixed.reshape(4, 2, 192, 384)

    def grad_block(s, c):
        ty = (y + s) % 4
        q = (ty // 2) * 2 + (co + c) % 2
        rows = lax.dynamic_index_in_dim(mixed, ty % 2, 1, keepdims=False).reshape(768, 384)
        columns = lax.dynamic_slice_in_dim(right, q * 384, 384, axis=0)
        return dot(rows, columns, ((1,), (1,))).astype(BF).reshape(4, 192, 384)

    halves = []
    for c in (0, 1):
        total = 0.0
        for s in (1, 3, 2, 0):
            block = grad_block(s, c)
            if (s, c) != (0, 0):
                block = moved(
                    block, lambda x, y, co, z, s=s, c=c: (x, y + s, (co + c) % 2, z)
                )
            total = total + block.astype(F32)
        halves.append(total)
    first = jnp.where(co == 0, halves[0], halves[1])
    second = jnp.where(co == 0, halves[1], halves[0])
    whole = jnp.concatenate([first, second], axis=0)
    return jnp.transpose(whole, (1, 0, 2))[None]


def solution(mesh):
    fine = Mesh(mesh.devices.reshape(4, 2, 2, 2, 4), AXES)
    cores = P("x", ("yl", "z"), None, ("yh", "co"))
    env = P(("yl", "z"), ("yh", "co"))
    return jax.shard_map(
        on_device,
        mesh=fine,
        in_specs=(cores, cores, env, env),
        out_specs=cores,
        check_vma=False,
    )
```

```python
import jax
import jax.numpy as jnp
from jax import lax
from jax.experimental import pallas as pl
from jax.experimental.pallas import tpu as pltpu
from jax.sharding import Mesh, PartitionSpec as P


AXES = ("x", "yh", "co", "yl", "z")
BF = jnp.bfloat16
F32 = jnp.float32
VMEM = pl.BlockSpec(memory_space=pltpu.VMEM)
SMEM = pl.BlockSpec(memory_space=pltpu.SMEM)
ANY = pl.BlockSpec(memory_space=pl.ANY)
SHIFTS = (0, 1, 3, 2)
LIMIT = pltpu.CompilerParams(vmem_limit_bytes=24 * 2**20)


def index_of(x, y, co, z):
    return (((x * 2 + y // 2) * 2 + co) * 2 + y % 2) * 4 + z


def moved(value, where):
    pairs = []
    for x in range(4):
        for y in range(4):
            for co in range(2):
                for z in range(4):
                    to = where(x, y, co, z)
                    if to is not None:
                        tx, ty, tc, tz = to
                        pairs.append((index_of(x, y, co, z), index_of(tx, ty % 4, tc, tz % 4)))
    return lax.ppermute(value, AXES, pairs)


def on_chip(value):
    return moved(value, lambda x, y, co, z: (x, y, 1 - co, z))


def exchanged(value, groups):
    return lax.all_to_all(value, AXES, 0, 0, axis_index_groups=groups, tiled=True)


def rings(t, left_along_y):
    groups = []
    for x in range(4):
        along_y = left_along_y != (x == 3 - t)
        for c in range(2):
            for other in range(4):
                groups.append([
                    index_of(x, k, c, other) if along_y else index_of(x, other, c, k)
                    for k in range(4)
                ])
    return groups


def dot(a, b, dims):
    return lax.dot_general(a, b, (dims, ((), ())), preferred_element_type=F32)


def shape_of(*shape, dtype=BF):
    return jax.ShapeDtypeStruct(shape, dtype)


def rows(start, size):
    return pl.ds(pl.multiple_of(start, size), size)


def put_left(co, own_ref, other_ref, left_s):
    for h, ref in ((co, own_ref), (1 - co, other_ref)):
        for j in range(4):
            left_s[rows(h * 192, 192), j * 384:(j + 1) * 384] = ref[j]


def placed(shape, pieces, table, slot):
    def kernel(table_ref, *refs):
        out, sems = refs[5:]
        ins = [[ref.at[half] for half in range(2)] for ref in refs[:3]]
        ins.append([refs[3].at[0], refs[4].at[0]])
        copies = [
            pltpu.make_async_copy(
                ins[n][half], out.at[slot(table_ref, n, half)], sems.at[2 * n + half]
            )
            for n in range(4) for half in range(2)
        ]
        for copy in copies:
            copy.start()
        for copy in copies:
            copy.wait()

    return pl.pallas_call(
        kernel,
        out_shape=shape_of(*shape),
        in_specs=[SMEM] + [ANY] * 5,
        out_specs=VMEM,
        scratch_shapes=[pltpu.SemaphoreType.DMA((8,))],
        compiler_params=LIMIT,
    )(table, *pieces[:3], *pieces[3])


def chain_step(scalars, own, other, x_full, y_full):
    def kernel(scalars_ref, own_ref, other_ref, x_ref, y_ref,
               theirs_ref, mine_ref, mixed_ref, right_ref, left_s, sum_l, sum_r):
        role, co = scalars_ref[0], scalars_ref[1]
        halves = ((co, mine_ref), (1 - co, theirs_ref))

        @pl.when(role == 1)
        def _():
            put_left(co, own_ref, other_ref, left_s)
            for i in range(4):
                mixed_ref[i] = dot(left_s[...], y_ref[i], ((1,), (0,))).astype(BF)
            sum_l[...] = dot(
                x_ref[...].reshape(1536, 1536), mixed_ref[...].reshape(1536, 384), ((0,), (0,))
            )
            for h, to in halves:
                for j in range(4):
                    to[j] = sum_l[rows(h * 768 + j * 192, 192), :].astype(to.dtype)

        @pl.when(role == 2)
        def _():
            for h, ref in ((co, own_ref), (1 - co, other_ref)):
                for j in range(4):
                    right_ref[rows(h * 768 + j * 192, 192), :] = ref[j]
            for i in range(4):
                image = dot(x_ref[i], right_ref[...], ((1,), (0,))).astype(BF)
                part = dot(image, y_ref[i], ((1,), (1,)))
                sum_r[...] = part if i == 0 else sum_r[...] + part
            for h, to in halves:
                for j in range(4):
                    to[j] = sum_r[rows(h * 192, 192), j * 384:(j + 1) * 384].astype(to.dtype)

    return pl.pallas_call(
        kernel,
        out_shape=(
            shape_of(4, 192, 384),
            shape_of(4, 192, 384),
            shape_of(4, 384, 384),
            shape_of(1536, 384),
        ),
        in_specs=[SMEM] + [VMEM] * 4,
        out_specs=(VMEM,) * 4,
        scratch_shapes=[
            pltpu.VMEM((384, 1536), BF),
            pltpu.VMEM((1536, 384), F32),
            pltpu.VMEM((384, 1536), F32),
        ],
        compiler_params=LIMIT,
    )(scalars, own, other, x_full, y_full)


def ordered(me, pieces):
    def kernel(me_ref, *refs):
        for s, ref in zip(SHIFTS, refs[:4]):
            refs[4][(me_ref[0] + 4 - s) % 4] = ref[...]

    return pl.pallas_call(
        kernel,
        out_shape=shape_of(4, *pieces[0].shape),
        in_specs=[SMEM] + [VMEM] * 4,
        out_specs=VMEM,
        compiler_params=LIMIT,
    )(me.reshape(1).astype(jnp.int32), *pieces)


def late_part(scalars, own, other, y_full, mixed_parts):
    def kernel(scalars_ref, own_ref, other_ref, *refs):
        y_ref, out_ref, env_s, m_s, m_sems = refs[0], *refs[5:]
        role, co, z = scalars_ref[0], scalars_ref[1], scalars_ref[2]
        of_m = [pltpu.make_async_copy(refs[1 + n], m_s.at[n], m_sems.at[n]) for n in range(4)]

        @pl.when(role == 1)
        def _():
            put_left(co, own_ref, other_ref, env_s)
            for i in range(4):
                out_ref[i] = dot(env_s[...], y_ref[i], ((1,), (0,))).astype(BF)

        @pl.when(role == 2)
        def _():
            for copy in of_m:
                copy.start()
            put_left(co, own_ref, other_ref, env_s)
            for n, s in enumerate(SHIFTS):
                of_m[n].wait()
                total = dot(m_s[n, 0], env_s[:, :384], ((1,), (1,)))
                for k in range(1, 4):
                    total += dot(m_s[n, k], env_s[:, k * 384:(k + 1) * 384], ((1,), (1,)))
                out_ref[(z + 4 - s) % 4] = total.astype(BF)

    return pl.pallas_call(
        kernel,
        out_shape=shape_of(4, 384, 384),
        in_specs=[SMEM] + [VMEM] * 3 + [ANY] * 4,
        out_specs=VMEM,
        scratch_shapes=[
            pltpu.VMEM((384, 1536), BF),
            pltpu.VMEM((4, 4, 384, 384), BF),
            pltpu.SemaphoreType.DMA((4,)),
        ],
        compiler_params=LIMIT,
    )(scalars, own, other, y_full, *mixed_parts)


def grad_part(scalars, late, mixed, right, right_other):
    def kernel(scalars_ref, *refs):
        late_r, mixed_r, right_r, other_r = refs[:4], refs[4], refs[5:9], refs[9:13]
        out_ref, mixed_s, right_s, sems = refs[13:]
        role, co = scalars_ref[0], scalars_ref[1]
        z, y = scalars_ref[2], scalars_ref[3]
        ring = jnp.where(role == 1, y, z)

        def fetched(copies):
            for copy in copies:
                copy.start()
            for copy in copies:
                copy.wait()

        def late_copies():
            return [
                pltpu.make_async_copy(late_r[n], mixed_s.at[(ring + 4 - s) % 4], sems.at[n])
                for n, s in enumerate(SHIFTS)
            ]

        def right_copies():
            return [
                pltpu.make_async_copy(
                    side[n], right_s.at[h, (y + 4 - s) % 4], sems.at[4 + 4 * k + n]
                )
                for k, (h, side) in enumerate(((co, right_r), (1 - co, other_r)))
                for n, s in enumerate(SHIFTS)
            ]

        @pl.when(role == 2)
        def _():
            fetched(late_copies())
            for q in range(4):
                columns = slice((q // 2) * 192, (q // 2) * 192 + 192)
                block = jnp.concatenate(
                    [mixed_s[2 * (q % 2) + e][:, columns] for e in range(2)], axis=1
                )
                out_ref[2 * q] = block[:192]
                out_ref[2 * q + 1] = block[192:]

        @pl.when(role == 1)
        def _():
            fetched(late_copies() + right_copies())

        @pl.when(role == 0)
        def _():
            fetched([pltpu.make_async_copy(mixed_r, mixed_s, sems.at[0])] + right_copies())

        @pl.when(role != 2)
        def _():
            for q in range(4):
                h, r = q // 2, (q % 2) * 384
                total = dot(mixed_s[0], right_s[h, 0, r:r + 384], ((1,), (1,)))
                for k in range(1, 4):
                    total += dot(mixed_s[k], right_s[h, k, r:r + 384], ((1,), (1,)))
                total = total.astype(BF)
                out_ref[2 * q] = total[:192]
                out_ref[2 * q + 1] = total[192:]

    return pl.pallas_call(
        kernel,
        out_shape=shape_of(8, 192, 384),
        in_specs=[SMEM] + [ANY] * 13,
        out_specs=VMEM,
        scratch_shapes=[
            pltpu.VMEM((4, 384, 384), BF),
            pltpu.VMEM((2, 4, 768, 384), BF),
            pltpu.SemaphoreType.DMA((12,)),
        ],
        compiler_params=LIMIT,
    )(scalars, *late, mixed, *right, *right_other)


def on_device(cores_x, cores_y, left_env, right_env):
    site = lax.axis_index("x")
    yh, yl = lax.axis_index("yh"), lax.axis_index("yl")
    co, z = lax.axis_index("co"), lax.axis_index("z")
    y = 2 * yh + yl

    def role_at(t):
        role = jnp.where(site == t, 1, jnp.where(site == 3 - t, 2, 0))
        return jnp.stack([role, co, z, y]).astype(jnp.int32)

    def half(core, which):
        return jnp.transpose(lax.dynamic_slice_in_dim(core[0], which * 4, 4, axis=1), (1, 0, 2))

    def turned(x, y, co, z):
        return x, (y // 2) * 2 + co, y % 2, z

    def turned_other(x, y, co, z):
        return x, (y // 2) * 2 + co, 1 - y % 2, z

    y_a, y_b = half(cores_y, yl), half(cores_y, 1 - yl)
    x_own, x_out = half(cores_x, co), half(cores_x, 1 - co)
    env = jnp.where(site == 0, left_env, right_env)

    def first_env(s):
        def to(x, y, co, z):
            home = (y // 2) * 2 + co
            if x == 0:
                return x, home + s, y % 2, z
            if x == 3:
                return x, home, y % 2, z + s
            return None

        return to

    own = [moved(env, first_env(s)) for s in SHIFTS]
    y_a, y_b, x_out, own = lax.optimization_barrier((y_a, y_b, x_out, own))
    y_a, y_b = moved(y_a, turned), moved(y_b, turned_other)
    x_other = on_chip(x_out)
    y_pair, x_pair = lax.optimization_barrier(
        (jnp.stack([y_a, y_b]), jnp.stack([x_own, x_other]))
    )

    def up_z(x, y, co, z):
        return x, y, co, z + 1

    def down_z(x, y, co, z):
        return x, y, co, z - 1

    def up_y(x, y, co, z):
        return x, y + 1, co, z

    def down_y(x, y, co, z):
        return x, y - 1, co, z

    def spread(pair, up, down):
        after, before = moved(pair, down), moved(pair, up)
        return [pair, after, before, (moved(before[:1], up), moved(after[1:], down))]

    y_parts = spread(y_pair, up_z, down_z)
    x_parts = spread(x_pair, up_y, down_y)
    table = jnp.stack([co, 1 - co] + [(z + s) % 4 for s in SHIFTS]).astype(jnp.int32)
    y_full = placed(
        (4, 2, 4, 192, 384), y_parts, table,
        lambda ref, n, half: (slice(None), ref[half], ref[2 + n]),
    ).reshape(4, 1536, 384)
    table = jnp.stack(
        [co * 384, (1 - co) * 384]
        + [((y + s) % 2) * 192 for s in SHIFTS]
        + [(((y + s) % 4) // 2) * 768 for s in SHIFTS]
    ).astype(jnp.int32)
    x_full = placed(
        (4, 384, 1536), x_parts, table,
        lambda ref, n, half: (
            slice(None), rows(ref[2 + n], 192),
            pl.ds(pl.multiple_of(ref[6 + n] + ref[half], 384), 384),
        ),
    )
    own = ordered(jnp.where(site == 0, y, z), own)
    other = on_chip(own)

    mixed, right = 0, 0
    for t in range(3):
        if t > 0:
            own = exchanged(jnp.broadcast_to(piece, (4, 192, 384)), rings(t, True))
            other = on_chip(own)
        theirs, mine, mixed_now, right_now = chain_step(role_at(t), own, other, x_full, y_full)
        mixed = mixed_now if t == 0 else jnp.where(site == t, mixed_now, mixed)
        right = right_now if t == 0 else jnp.where(site == 3 - t, right_now, right)
        both = (mine.astype(F32) + on_chip(theirs).astype(F32)).astype(BF)
        both = exchanged(both, rings(t, False))
        total = jnp.sum(both.astype(F32), axis=0).astype(BF)

        def hop(x, y, co, z):
            if x == t:
                return x + 1, y, co, z
            if x == 3 - t:
                return x - 1, y, co, z
            return None

        piece = moved(total, hop)

    mixed, right, _ = lax.optimization_barrier((mixed, right, total))

    def along_y(value, s, planes):
        return moved(value, lambda x, y, co, z: (x, y + s, co, z) if x in planes else None)

    def block(stack, n):
        return lax.dynamic_index_in_dim(stack, n % 4, 0, keepdims=False)

    mixed = [block(mixed, y)] + [along_y(block(mixed, y + s), s, (0, 1, 2, 3)) for s in SHIFTS[1:]]
    right_own = lax.dynamic_slice_in_dim(right, co * 768, 768, axis=0)
    right_own = [right_own] + [along_y(right_own, s, (0, 1, 2, 3)) for s in SHIFTS[1:]]
    right_other = [on_chip(part) for part in right_own]
    mixed = ordered(y, mixed)
    mixed_parts = [mixed] + [
        moved(mixed, lambda x, y, co, z, s=s: (x, y, co, z + s) if x == 0 else None)
        for s in SHIFTS[1:]
    ]

    own = ordered(y, [piece] + [along_y(piece, s, (0, 3)) for s in SHIFTS[1:]])
    other = on_chip(own)
    late = late_part(role_at(3), own, other, y_full, mixed_parts)
    ring = jnp.where(site == 3, y, z)

    def late_to(s):
        def to(x, y, co, z):
            if x == 3:
                return x, y + s, co, z
            if x == 0:
                return x, y, co, z + s
            return None

        return to

    late = [block(late, ring)] + [moved(block(late, ring + s), late_to(s)) for s in SHIFTS[1:]]
    grad = grad_part(role_at(3), late, mixed, right_own, right_other)
    grad = lax.all_to_all(grad, ("yh", "co", "yl"), 0, 0, tiled=True)
    grad = grad.reshape(2, 2, 2, 192, 384).transpose(3, 1, 0, 2, 4).reshape(1, 192, 8, 384)
    return grad.astype(F32)


def solution(mesh):
    fine = Mesh(mesh.devices.reshape(4, 2, 2, 2, 4), AXES)
    cores = P("x", ("yl", "z"), None, ("yh", "co"))
    env = P(("yl", "z"), ("yh", "co"))

    return jax.shard_map(
        on_device,
        mesh=fine,
        in_specs=(cores, cores, env, env),
        out_specs=cores,
        check_vma=False,
    )
```

```python
import jax
import jax.numpy as jnp
from jax import lax
from jax.experimental import pallas as pl
from jax.experimental.pallas import tpu as pltpu
from jax.sharding import Mesh, PartitionSpec as P


AXES = ("x", "yh", "co", "yl", "z")
BF = jnp.bfloat16
F32 = jnp.float32
VMEM = pl.BlockSpec(memory_space=pltpu.VMEM)
SMEM = pl.BlockSpec(memory_space=pltpu.SMEM)
ANY = pl.BlockSpec(memory_space=pl.ANY)
HBM = pl.BlockSpec(memory_space=pltpu.HBM)
SHIFTS = (0, 1, 3, 2)
LIMIT = pltpu.CompilerParams(vmem_limit_bytes=24 * 2**20)


def index_of(x, y, co, z):
    return (((x * 2 + y // 2) * 2 + co) * 2 + y % 2) * 4 + z


def moved(value, where):
    pairs = []
    for x in range(4):
        for y in range(4):
            for co in range(2):
                for z in range(4):
                    to = where(x, y, co, z)
                    if to is not None:
                        tx, ty, tc, tz = to
                        pairs.append((index_of(x, y, co, z), index_of(tx, ty % 4, tc, tz % 4)))
    return lax.ppermute(value, AXES, pairs)


def on_chip(value):
    return moved(value, lambda x, y, co, z: (x, y, 1 - co, z))


def exchanged(value, groups):
    return lax.all_to_all(value, AXES, 0, 0, axis_index_groups=groups, tiled=True)


def rings(t, left_along_y):
    groups = []
    for x in range(4):
        along_y = left_along_y != (x == 3 - t)
        for c in range(2):
            for other in range(4):
                groups.append([
                    index_of(x, k, c, other) if along_y else index_of(x, other, c, k)
                    for k in range(4)
                ])
    return groups


def dot(a, b, dims):
    return lax.dot_general(a, b, (dims, ((), ())), preferred_element_type=F32)


def shape_of(*shape, dtype=BF):
    return jax.ShapeDtypeStruct(shape, dtype)


def rows(start, size):
    return pl.ds(pl.multiple_of(start, size), size)


def put_left(co, own_ref, other_ref, left_s):
    for h, ref in ((co, own_ref), (1 - co, other_ref)):
        for j in range(4):
            left_s[rows(h * 192, 192), j * 384:(j + 1) * 384] = ref[j]


def placed(shape, scalars, pieces, slot):
    def kernel(scalars_ref, *refs):
        out, sems = refs[8:]
        copies = [
            pltpu.make_async_copy(
                refs[2 * n + half], out.at[slot(scalars_ref, s, half)], sems.at[2 * n + half]
            )
            for n, s in enumerate(SHIFTS) for half in range(2)
        ]
        for copy in copies:
            copy.start()
        for copy in copies:
            copy.wait()

    return pl.pallas_call(
        kernel,
        out_shape=shape_of(*shape),
        in_specs=[SMEM] + [ANY] * 8,
        out_specs=VMEM,
        scratch_shapes=[pltpu.SemaphoreType.DMA((8,))],
        compiler_params=LIMIT,
    )(scalars, *pieces)


def summed(parts):
    def kernel(parts_ref, out_ref):
        total = parts_ref[0].astype(F32)
        for n in range(1, 4):
            total += parts_ref[n].astype(F32)
        out_ref[...] = total.astype(BF)

    return pl.pallas_call(
        kernel,
        out_shape=shape_of(192, 384),
        in_specs=[VMEM],
        out_specs=VMEM,
        compiler_params=LIMIT,
    )(parts)


def added(first, second):
    def kernel(first_ref, second_ref, out_ref):
        for n in range(4):
            out_ref[n] = (first_ref[n].astype(F32) + second_ref[n].astype(F32)).astype(BF)

    return pl.pallas_call(
        kernel,
        out_shape=shape_of(4, 192, 384),
        in_specs=[VMEM] * 2,
        out_specs=VMEM,
        compiler_params=LIMIT,
    )(first, second)


def early_part(scalars, mixed, right):
    def kernel(scalars_ref, *refs):
        mixed_r, right_r, outs, half_ref, mixed_s, sems = (
            refs[:3], refs[3:6], refs[6:10], refs[10], refs[11], refs[12]
        )
        site, co, y = scalars_ref[0], scalars_ref[1], scalars_ref[3]
        half = rows(co * 768, 768)
        for t in range(3):
            @pl.when(site == t)
            def _():
                pltpu.make_async_copy(mixed_r[t], mixed_s, sems.at[0]).start()

            @pl.when(site == 3 - t)
            def _():
                pltpu.make_async_copy(right_r[t].at[half], half_ref, sems.at[1]).start()

        @pl.when(site < 3)
        def _():
            pltpu.make_async_copy(mixed_r[0], mixed_s, sems.at[0]).wait()
            for s, out in zip(SHIFTS, outs):
                out[...] = mixed_s[(y + s) % 4]

        @pl.when(site > 0)
        def _():
            pltpu.make_async_copy(right_r[0].at[half], half_ref, sems.at[1]).wait()

    outs = pl.pallas_call(
        kernel,
        out_shape=(shape_of(384, 384),) * 4 + (shape_of(768, 384),),
        in_specs=[SMEM] + [HBM] * 6,
        out_specs=(VMEM,) * 5,
        scratch_shapes=[pltpu.VMEM((4, 384, 384), BF), pltpu.SemaphoreType.DMA((2,))],
        compiler_params=LIMIT,
    )(scalars, *mixed, *right)
    return outs[:4], outs[4]


def chain_step(t, scalars, own, other, x_full, y_full):
    def kernel(scalars_ref, own_ref, other_ref, x_ref, y_ref,
               theirs_ref, mine_ref, mixed_out, right_out,
               left_s, sum_l, sum_r, mixed_ref, right_ref, sem):
        site, co = scalars_ref[0], scalars_ref[1]
        halves = ((co, mine_ref), (1 - co, theirs_ref))

        @pl.when(site == t)
        def _():
            put_left(co, own_ref, other_ref, left_s)
            for i in range(4):
                mixed_ref[i] = dot(left_s[...], y_ref[i], ((1,), (0,))).astype(BF)
            keep = pltpu.make_async_copy(mixed_ref, mixed_out, sem)
            keep.start()
            sum_l[...] = dot(
                x_ref[...].reshape(1536, 1536), mixed_ref[...].reshape(1536, 384), ((0,), (0,))
            )
            for h, to in halves:
                for j in range(4):
                    to[j] = sum_l[rows(h * 768 + j * 192, 192), :].astype(to.dtype)
            keep.wait()

        @pl.when(site == 3 - t)
        def _():
            for h, ref in ((co, own_ref), (1 - co, other_ref)):
                for j in range(4):
                    right_ref[rows(h * 768 + j * 192, 192), :] = ref[j]
            keep = pltpu.make_async_copy(right_ref, right_out, sem)
            keep.start()
            for i in range(4):
                image = dot(x_ref[i], right_ref[...], ((1,), (0,))).astype(BF)
                part = dot(image, y_ref[i], ((1,), (1,)))
                sum_r[...] = part if i == 0 else sum_r[...] + part
            for h, to in halves:
                for j in range(4):
                    to[j] = sum_r[rows(h * 192, 192), j * 384:(j + 1) * 384].astype(to.dtype)
            keep.wait()

    return pl.pallas_call(
        kernel,
        out_shape=(
            shape_of(4, 192, 384),
            shape_of(4, 192, 384),
            shape_of(4, 384, 384),
            shape_of(1536, 384),
        ),
        in_specs=[SMEM] + [VMEM] * 4,
        out_specs=(VMEM, VMEM, HBM, HBM),
        scratch_shapes=[
            pltpu.VMEM((384, 1536), BF),
            pltpu.VMEM((1536, 384), F32),
            pltpu.VMEM((384, 1536), F32),
            pltpu.VMEM((4, 384, 384), BF),
            pltpu.VMEM((1536, 384), BF),
            pltpu.SemaphoreType.DMA,
        ],
        compiler_params=LIMIT,
    )(scalars, own, other, x_full, y_full)


def ordered(scalars, pieces):
    def kernel(scalars_ref, *refs):
        me = jnp.where(scalars_ref[4] == 1, scalars_ref[2], scalars_ref[3])
        for s, ref in zip(SHIFTS, refs[:4]):
            refs[4][(me + 4 - s) % 4] = ref[...]

    return pl.pallas_call(
        kernel,
        out_shape=shape_of(4, *pieces[0].shape),
        in_specs=[SMEM] + [VMEM] * 4,
        out_specs=VMEM,
        compiler_params=LIMIT,
    )(scalars, *pieces)


def late_part(scalars, own, other, y_full, mixed_parts):
    def kernel(scalars_ref, own_ref, other_ref, *refs):
        y_ref, outs, env_s, m_s, m_sems = refs[0], refs[5:9], *refs[9:]
        site, co, y = scalars_ref[0], scalars_ref[1], scalars_ref[3]
        of_m = [pltpu.make_async_copy(refs[1 + n], m_s.at[n], m_sems.at[n]) for n in range(4)]

        @pl.when(site == 3)
        def _():
            put_left(co, own_ref, other_ref, env_s)
            for s, out in zip(SHIFTS, outs):
                out[...] = dot(env_s[...], y_ref[(y + s) % 4], ((1,), (0,))).astype(BF)

        @pl.when(site == 0)
        def _():
            for copy in of_m:
                copy.start()
            put_left(co, own_ref, other_ref, env_s)
            for n, s in enumerate(SHIFTS):
                of_m[n].wait()
                total = dot(m_s[n, 0], env_s[:, :384], ((1,), (1,)))
                for k in range(1, 4):
                    total += dot(m_s[n, k], env_s[:, k * 384:(k + 1) * 384], ((1,), (1,)))
                outs[SHIFTS.index((4 - s) % 4)][...] = total.astype(BF)

    return pl.pallas_call(
        kernel,
        out_shape=(shape_of(384, 384),) * 4,
        in_specs=[SMEM] + [VMEM] * 3 + [ANY] * 4,
        out_specs=(VMEM,) * 4,
        scratch_shapes=[
            pltpu.VMEM((384, 1536), BF),
            pltpu.VMEM((4, 4, 384, 384), BF),
            pltpu.SemaphoreType.DMA((4,)),
        ],
        compiler_params=LIMIT,
    )(scalars, own, other, y_full, *mixed_parts)


def grad_part(scalars, late, mixed, right, right_other):
    def kernel(scalars_ref, *refs):
        late_r, mixed_r, right_r, other_r = refs[:4], refs[4], refs[5:9], refs[9:13]
        out_ref, mixed_s, right_s, sems = refs[13:]
        site, co = scalars_ref[0], scalars_ref[1]
        z, y = scalars_ref[2], scalars_ref[3]
        ring = jnp.where(site == 3, y, z)

        def fetched(copies):
            for copy in copies:
                copy.start()
            for copy in copies:
                copy.wait()

        def late_copies():
            return [
                pltpu.make_async_copy(late_r[n], mixed_s.at[(ring + 4 - s) % 4], sems.at[n])
                for n, s in enumerate(SHIFTS)
            ]

        def right_copies():
            return [
                pltpu.make_async_copy(
                    side[n], right_s.at[h, (y + 4 - s) % 4], sems.at[4 + 4 * k + n]
                )
                for k, (h, side) in enumerate(((co, right_r), (1 - co, other_r)))
                for n, s in enumerate(SHIFTS)
            ]

        @pl.when(site == 0)
        def _():
            fetched(late_copies())
            for q in range(4):
                columns = slice((q // 2) * 192, (q // 2) * 192 + 192)
                block = jnp.concatenate(
                    [mixed_s[2 * (q % 2) + e][:, columns] for e in range(2)], axis=1
                )
                out_ref[2 * q] = block[:192]
                out_ref[2 * q + 1] = block[192:]

        @pl.when(site == 3)
        def _():
            fetched(late_copies() + right_copies())

        @pl.when((site == 1) | (site == 2))
        def _():
            fetched([pltpu.make_async_copy(mixed_r, mixed_s, sems.at[0])] + right_copies())

        @pl.when(site != 0)
        def _():
            for q in range(4):
                h, r = q // 2, (q % 2) * 384
                total = dot(mixed_s[0], right_s[h, 0, r:r + 384], ((1,), (1,)))
                for k in range(1, 4):
                    total += dot(mixed_s[k], right_s[h, k, r:r + 384], ((1,), (1,)))
                total = total.astype(BF)
                out_ref[2 * q] = total[:192]
                out_ref[2 * q + 1] = total[192:]

    return pl.pallas_call(
        kernel,
        out_shape=shape_of(8, 192, 384),
        in_specs=[SMEM] + [ANY] * 13,
        out_specs=VMEM,
        scratch_shapes=[
            pltpu.VMEM((4, 384, 384), BF),
            pltpu.VMEM((2, 4, 768, 384), BF),
            pltpu.SemaphoreType.DMA((12,)),
        ],
        compiler_params=LIMIT,
    )(scalars, *late, mixed, *right, *right_other)


def on_device(cores_x, cores_y, left_env, right_env):
    site = lax.axis_index("x")
    yh, yl = lax.axis_index("yh"), lax.axis_index("yl")
    co, z = lax.axis_index("co"), lax.axis_index("z")
    y = 2 * yh + yl

    scalars = jnp.stack([site, co, z, y, site // 3]).astype(jnp.int32)
    along = jnp.stack([site, co, z, y, 0]).astype(jnp.int32)

    def half(core, which):
        return jnp.transpose(lax.dynamic_slice_in_dim(core[0], which * 4, 4, axis=1), (1, 0, 2))

    def turned(x, y, co, z):
        return x, (y // 2) * 2 + co, y % 2, z

    def turned_other(x, y, co, z):
        return x, (y // 2) * 2 + co, 1 - y % 2, z

    y_a, y_b = half(cores_y, yl), half(cores_y, 1 - yl)
    x_own, x_out = half(cores_x, co), half(cores_x, 1 - co)
    env = jnp.where(site == 0, left_env, right_env)

    def first_env(s):
        def to(x, y, co, z):
            home = (y // 2) * 2 + co
            if x == 0:
                return x, home + s, y % 2, z
            if x == 3:
                return x, home, y % 2, z + s
            return None

        return to

    own = [moved(env, first_env(s)) for s in SHIFTS]
    y_a, y_b, x_out, own = lax.optimization_barrier((y_a, y_b, x_out, own))
    y_a, y_b = moved(y_a, turned), moved(y_b, turned_other)
    x_other = on_chip(x_out)
    y_a, y_b, x_own, x_other = lax.optimization_barrier((y_a, y_b, x_own, x_other))

    def up_z(x, y, co, z):
        return x, y, co, z + 1

    def down_z(x, y, co, z):
        return x, y, co, z - 1

    def up_y(x, y, co, z):
        return x, y + 1, co, z

    def down_y(x, y, co, z):
        return x, y - 1, co, z

    def spread(first, second, up, down):
        before, after = moved(first, up), moved(second, down)
        first_after, second_before = moved(first, down), moved(second, up)
        across = moved(before, up), moved(after, down)
        return [first, second, first_after, after, before, second_before, *across]

    y_parts = spread(y_a, y_b, up_z, down_z)
    x_parts = spread(x_own, x_other, up_y, down_y)
    y_full = placed(
        (4, 2, 4, 192, 384), scalars, y_parts,
        lambda ref, s, half: (
            slice(None), ref[1] if half == 0 else 1 - ref[1], (ref[2] + s) % 4
        ),
    ).reshape(4, 1536, 384)

    def x_slot(ref, s, half):
        from_y = (ref[3] + s) % 4
        quarter = (from_y // 2) * 2 + (ref[1] if half == 0 else 1 - ref[1])
        return slice(None), rows((from_y % 2) * 192, 192), rows(quarter * 384, 384)

    x_full = placed((4, 384, 1536), scalars, x_parts, x_slot)
    own = ordered(scalars, own)
    other = on_chip(own)

    mixed, right = [], []
    for t in range(3):
        if t > 0:
            own = exchanged(jnp.broadcast_to(piece, (4, 192, 384)), rings(t, True))
            other = on_chip(own)
        theirs, mine, mixed_now, right_now = chain_step(t, scalars, own, other, x_full, y_full)
        mixed.append(mixed_now)
        right.append(right_now)
        total = summed(exchanged(added(mine, on_chip(theirs)), rings(t, False)))

        def hop(x, y, co, z):
            if x == t:
                return x + 1, y, co, z
            if x == 3 - t:
                return x - 1, y, co, z
            return None

        piece = moved(total, hop)

    mixed[2], _ = lax.optimization_barrier((mixed[2], total))

    def along_y(value, s, planes):
        return moved(value, lambda x, y, co, z: (x, y + s, co, z) if x in planes else None)

    blocks, right_own = early_part(along, mixed, right)
    mixed = [blocks[0]] + [
        along_y(block, s, (0, 1, 2, 3)) for s, block in zip(SHIFTS[1:], blocks[1:])
    ]
    right_own = [right_own] + [along_y(right_own, s, (0, 1, 2, 3)) for s in SHIFTS[1:]]
    right_other = [on_chip(part) for part in right_own]
    mixed = ordered(along, mixed)
    mixed_parts = [mixed] + [
        moved(mixed, lambda x, y, co, z, s=s: (x, y, co, z + s) if x == 0 else None)
        for s in SHIFTS[1:]
    ]

    own = ordered(along, [piece] + [along_y(piece, s, (0, 3)) for s in SHIFTS[1:]])
    other = on_chip(own)
    late = late_part(along, own, other, y_full, mixed_parts)

    def late_to(s):
        def to(x, y, co, z):
            if x == 3:
                return x, y + s, co, z
            if x == 0:
                return x, y, co, z + s
            return None

        return to

    late = [late[0]] + [moved(part, late_to(s)) for s, part in zip(SHIFTS[1:], late[1:])]
    grad = grad_part(along, late, mixed, right_own, right_other)
    grad = lax.all_to_all(grad, ("yh", "co", "yl"), 0, 0, tiled=True)
    grad = grad.reshape(2, 2, 2, 192, 384).transpose(3, 1, 0, 2, 4).reshape(1, 192, 8, 384)
    return grad.astype(F32)


def solution(mesh):
    fine = Mesh(mesh.devices.reshape(4, 2, 2, 2, 4), AXES)
    cores = P("x", ("yl", "z"), None, ("yh", "co"))
    env = P(("yl", "z"), ("yh", "co"))

    return jax.shard_map(
        on_device,
        mesh=fine,
        in_specs=(cores, cores, env, env),
        out_specs=cores,
        check_vma=False,
    )
```

```python
import jax
import jax.numpy as jnp
from jax import lax
from jax.experimental import pallas as pl
from jax.experimental.pallas import tpu as pltpu
from jax.sharding import Mesh, PartitionSpec as P


AXES = ("x", "yh", "co", "yl", "z")
BF = jnp.bfloat16
F32 = jnp.float32
VMEM = pl.BlockSpec(memory_space=pltpu.VMEM)
SMEM = pl.BlockSpec(memory_space=pltpu.SMEM)
ANY = pl.BlockSpec(memory_space=pl.ANY)
HBM = pl.BlockSpec(memory_space=pltpu.HBM)
SHIFTS = (0, 1, 3, 2)
LIMIT = pltpu.CompilerParams(vmem_limit_bytes=24 * 2**20)


def index_of(x, y, co, z):
    return (((x * 2 + y // 2) * 2 + co) * 2 + y % 2) * 4 + z


def moved(value, where):
    pairs = []
    for x in range(4):
        for y in range(4):
            for co in range(2):
                for z in range(4):
                    to = where(x, y, co, z)
                    if to is not None:
                        tx, ty, tc, tz = to
                        pairs.append((index_of(x, y, co, z), index_of(tx, ty % 4, tc, tz % 4)))
    return lax.ppermute(value, AXES, pairs)


def on_chip(value, planes=(0, 1, 2, 3)):
    return moved(value, lambda x, y, co, z: (x, y, 1 - co, z) if x in planes else None)


def exchanged(value, groups):
    return lax.all_to_all(value, AXES, 0, 0, axis_index_groups=groups, tiled=True)


def rings(t, left_along_y):
    groups = []
    for x in range(4):
        along_y = left_along_y != (x == 3 - t) or (t > 0 and x in (0, 3) and t < 3)
        for c in range(2):
            for other in range(4):
                groups.append([
                    index_of(x, k, c, other) if along_y else index_of(x, other, c, k)
                    for k in range(4)
                ])
    return groups


def dot(a, b, dims):
    return lax.dot_general(a, b, (dims, ((), ())), preferred_element_type=F32)


def shape_of(*shape, dtype=BF):
    return jax.ShapeDtypeStruct(shape, dtype)


def rows(start, size):
    return pl.ds(pl.multiple_of(start, size), size)


def put_left(co, own_ref, other_ref, left_s):
    for h, ref in ((co, own_ref), (1 - co, other_ref)):
        for j in range(4):
            left_s[rows(h * 192, 192), j * 384:(j + 1) * 384] = ref[j]


def placed(shape, scalars, pieces, slot):
    def kernel(scalars_ref, *refs):
        out, sems = refs[8:]
        copies = [
            pltpu.make_async_copy(
                refs[2 * n + half], out.at[slot(scalars_ref, s, half)], sems.at[2 * n + half]
            )
            for n, s in enumerate(SHIFTS) for half in range(2)
        ]
        for copy in copies:
            copy.start()
        for copy in copies:
            copy.wait()

    return pl.pallas_call(
        kernel,
        out_shape=shape_of(*shape),
        in_specs=[SMEM] + [ANY] * 8,
        out_specs=VMEM,
        scratch_shapes=[pltpu.SemaphoreType.DMA((8,))],
        compiler_params=LIMIT,
    )(scalars, *pieces)


def summed(parts):
    def kernel(parts_ref, out_ref):
        total = parts_ref[0].astype(F32)
        for n in range(1, 4):
            total += parts_ref[n].astype(F32)
        out_ref[...] = total.astype(BF)

    return pl.pallas_call(
        kernel,
        out_shape=shape_of(192, 384),
        in_specs=[VMEM],
        out_specs=VMEM,
        compiler_params=LIMIT,
    )(parts)


def added(first, second):
    def kernel(first_ref, second_ref, out_ref):
        for n in range(4):
            out_ref[n] = (first_ref[n].astype(F32) + second_ref[n].astype(F32)).astype(BF)

    return pl.pallas_call(
        kernel,
        out_shape=shape_of(4, 192, 384),
        in_specs=[VMEM] * 2,
        out_specs=VMEM,
        compiler_params=LIMIT,
    )(first, second)


def early_part(scalars, mixed, right):
    def kernel(scalars_ref, *refs):
        count = len(mixed) + len(right)
        outs, half_ref, mixed_s, sems = refs[count:count + 4], *refs[count + 4:]
        site, co, y = scalars_ref[0], scalars_ref[1], scalars_ref[3]
        mixed_r = list(zip(mixed, refs[:len(mixed)]))
        right_r = list(zip(right, refs[len(mixed):count]))
        half = rows(co * 768, 768)
        for at, ref in right_r:
            @pl.when(site == at)
            def _():
                copy = pltpu.make_async_copy(ref.at[half], half_ref, sems.at[1])
                copy.start()
                copy.wait()
        for at, ref in mixed_r:
            @pl.when(site == at)
            def _():
                copy = pltpu.make_async_copy(ref, mixed_s, sems.at[0])
                copy.start()
                copy.wait()
                for s, out in zip(SHIFTS, outs):
                    out[...] = mixed_s[(y + s) % 4]

    outs = pl.pallas_call(
        kernel,
        out_shape=(shape_of(384, 384),) * 4 + (shape_of(768, 384),),
        in_specs=[SMEM] + [ANY] * (len(mixed) + len(right)),
        out_specs=(VMEM,) * 5,
        scratch_shapes=[pltpu.VMEM((4, 384, 384), BF), pltpu.SemaphoreType.DMA((2,))],
        compiler_params=LIMIT,
    )(scalars, *mixed.values(), *right.values())
    return outs[:4], outs[4]


def chain_step(t, scalars, own, other, x_full, y_full):
    def kernel(scalars_ref, own_ref, other_ref, x_ref, y_ref,
               theirs_ref, mine_ref, mixed_out, right_out,
               left_s, sum_l, sum_r, mixed_ref, right_ref, sem):
        site, co = scalars_ref[0], scalars_ref[1]
        halves = ((co, mine_ref), (1 - co, theirs_ref))

        @pl.when(site == t)
        def _():
            put_left(co, own_ref, other_ref, left_s)
            for i in range(4):
                mixed_ref[i] = dot(left_s[...], y_ref[i], ((1,), (0,))).astype(BF)
            keep = pltpu.make_async_copy(mixed_ref, mixed_out, sem)
            keep.start()
            sum_l[...] = dot(
                x_ref[...].reshape(1536, 1536), mixed_ref[...].reshape(1536, 384), ((0,), (0,))
            )
            for h, to in halves:
                for j in range(4):
                    to[j] = sum_l[rows(h * 768 + j * 192, 192), :].astype(to.dtype)
            keep.wait()

        @pl.when(site == 3 - t)
        def _():
            for h, ref in ((co, own_ref), (1 - co, other_ref)):
                for j in range(4):
                    right_ref[rows(h * 768 + j * 192, 192), :] = ref[j]
            keep = pltpu.make_async_copy(right_ref, right_out, sem)
            keep.start()
            for i in range(4):
                image = dot(x_ref[i], right_ref[...], ((1,), (0,))).astype(BF)
                part = dot(image, y_ref[i], ((1,), (1,)))
                sum_r[...] = part if i == 0 else sum_r[...] + part
            for h, to in halves:
                for j in range(4):
                    to[j] = sum_r[rows(h * 192, 192), j * 384:(j + 1) * 384].astype(to.dtype)
            keep.wait()

    return pl.pallas_call(
        kernel,
        out_shape=(
            shape_of(4, 192, 384),
            shape_of(4, 192, 384),
            pltpu.HBM((4, 384, 384), BF),
            pltpu.HBM((1536, 384), BF),
        ),
        in_specs=[SMEM] + [VMEM] * 4,
        out_specs=(VMEM, VMEM, HBM, HBM),
        scratch_shapes=[
            pltpu.VMEM((384, 1536), BF),
            pltpu.VMEM((1536, 384), F32),
            pltpu.VMEM((384, 1536), F32),
            pltpu.VMEM((4, 384, 384), BF),
            pltpu.VMEM((1536, 384), BF),
            pltpu.SemaphoreType.DMA,
        ],
        compiler_params=LIMIT,
    )(scalars, own, other, x_full, y_full)


def ordered(scalars, pieces):
    def kernel(scalars_ref, *refs):
        me = jnp.where(scalars_ref[4] == 1, scalars_ref[2], scalars_ref[3])
        for s, ref in zip(SHIFTS, refs[:4]):
            refs[4][(me + 4 - s) % 4] = ref[...]

    return pl.pallas_call(
        kernel,
        out_shape=shape_of(4, *pieces[0].shape),
        in_specs=[SMEM] + [VMEM] * 4,
        out_specs=VMEM,
        compiler_params=LIMIT,
    )(scalars, *pieces)


def late_part(scalars, own, other, y_full, mixed_parts):
    def kernel(scalars_ref, own_ref, other_ref, *refs):
        y_ref, out_ref, env_s, m_s, m_sems = refs[0], *refs[5:]
        site, co, z = scalars_ref[0], scalars_ref[1], scalars_ref[2]
        of_m = [pltpu.make_async_copy(refs[1 + n], m_s.at[n], m_sems.at[n]) for n in range(4)]

        @pl.when(site == 3)
        def _():
            put_left(co, own_ref, other_ref, env_s)
            for i in range(4):
                out_ref[i] = dot(env_s[...], y_ref[i], ((1,), (0,))).astype(BF)

        @pl.when(site == 0)
        def _():
            for copy in of_m:
                copy.start()
            put_left(co, own_ref, other_ref, env_s)
            for n, s in enumerate(SHIFTS):
                of_m[n].wait()
                total = dot(m_s[n, 0], env_s[:, :384], ((1,), (1,)))
                for k in range(1, 4):
                    total += dot(m_s[n, k], env_s[:, k * 384:(k + 1) * 384], ((1,), (1,)))
                out_ref[(z + 4 - s) % 4] = total.astype(BF)

    return pl.pallas_call(
        kernel,
        out_shape=shape_of(4, 384, 384),
        in_specs=[SMEM] + [VMEM] * 3 + [ANY] * 4,
        out_specs=VMEM,
        scratch_shapes=[
            pltpu.VMEM((384, 1536), BF),
            pltpu.VMEM((4, 4, 384, 384), BF),
            pltpu.SemaphoreType.DMA((4,)),
        ],
        compiler_params=LIMIT,
    )(scalars, own, other, y_full, *mixed_parts)


def grad_part(scalars, late, mixed, right, right_other):
    def kernel(scalars_ref, *refs):
        late_r, mixed_r = refs[:2]
        out_ref, mixed_s, right_s, sems = refs[4:]
        site, co = scalars_ref[0], scalars_ref[1]

        def fetched(copies):
            for copy in copies:
                copy.start()
            for copy in copies:
                copy.wait()

        def late_copies():
            return [pltpu.make_async_copy(late_r, mixed_s, sems.at[0])]

        def right_copies(at):
            return [
                pltpu.make_async_copy(refs[at + k], right_s.at[h], sems.at[1 + k])
                for k, h in enumerate((co, 1 - co))
            ]

        @pl.when(site == 0)
        def _():
            fetched(late_copies())
            for q in range(4):
                columns = slice((q // 2) * 192, (q // 2) * 192 + 192)
                block = jnp.concatenate(
                    [mixed_s[2 * (q % 2) + e][:, columns] for e in range(2)], axis=1
                )
                out_ref[2 * q] = block[:192]
                out_ref[2 * q + 1] = block[192:]

        @pl.when(site == 3)
        def _():
            fetched(late_copies() + right_copies(2))

        @pl.when((site == 1) | (site == 2))
        def _():
            fetched([pltpu.make_async_copy(mixed_r, mixed_s, sems.at[0])] + right_copies(2))

        @pl.when(site != 0)
        def _():
            for q in range(4):
                h, r = q // 2, (q % 2) * 384
                total = dot(mixed_s[0], right_s[h, 0, r:r + 384], ((1,), (1,)))
                for k in range(1, 4):
                    total += dot(mixed_s[k], right_s[h, k, r:r + 384], ((1,), (1,)))
                total = total.astype(BF)
                out_ref[2 * q] = total[:192]
                out_ref[2 * q + 1] = total[192:]

    return pl.pallas_call(
        kernel,
        out_shape=shape_of(8, 192, 384),
        in_specs=[SMEM] + [ANY] * 4,
        out_specs=VMEM,
        scratch_shapes=[
            pltpu.VMEM((4, 384, 384), BF),
            pltpu.VMEM((2, 4, 768, 384), BF),
            pltpu.SemaphoreType.DMA((3,)),
        ],
        compiler_params=LIMIT,
    )(scalars, late, mixed, right, right_other)


def on_device(cores_x, cores_y, left_env, right_env):
    site = lax.axis_index("x")
    yh, yl = lax.axis_index("yh"), lax.axis_index("yl")
    co, z = lax.axis_index("co"), lax.axis_index("z")
    y = 2 * yh + yl

    scalars = jnp.stack([site, co, z, y, site // 3]).astype(jnp.int32)
    along = jnp.stack([site, co, z, y, 0]).astype(jnp.int32)

    def half(core, which):
        return jnp.transpose(lax.dynamic_slice_in_dim(core[0], which * 4, 4, axis=1), (1, 0, 2))

    def turned(x, y, co, z):
        return x, (y // 2) * 2 + co, y % 2, z

    def turned_other(x, y, co, z):
        return x, (y // 2) * 2 + co, 1 - y % 2, z

    y_a, y_b = half(cores_y, yl), half(cores_y, 1 - yl)
    x_own, x_out = half(cores_x, co), half(cores_x, 1 - co)
    env = jnp.where(site == 0, left_env, right_env)

    def first_env(s):
        def to(x, y, co, z):
            home = (y // 2) * 2 + co
            if x == 0:
                return x, home + s, y % 2, z
            if x == 3:
                return x, home, y % 2, z + s
            return None

        return to

    own = [moved(env, turned)] + [moved(env, first_env(s)) for s in SHIFTS[1:]]
    y_a, y_b, x_out, own = lax.optimization_barrier((y_a, y_b, x_out, own))
    y_a, y_b = moved(y_a, turned), moved(y_b, turned_other)
    x_other = on_chip(x_out)
    y_a, y_b, x_own, x_other = lax.optimization_barrier((y_a, y_b, x_own, x_other))

    def up_z(x, y, co, z):
        return x, y, co, z + 1

    def down_z(x, y, co, z):
        return x, y, co, z - 1

    def up_y(x, y, co, z):
        return x, y + 1, co, z

    def down_y(x, y, co, z):
        return x, y - 1, co, z

    def spread(first, second, up, down):
        before, after = moved(first, up), moved(second, down)
        first_after, second_before = moved(first, down), moved(second, up)
        across = moved(before, up), moved(after, down)
        return [first, second, first_after, after, before, second_before, *across]

    y_parts = spread(y_a, y_b, up_z, down_z)
    x_parts = spread(x_own, x_other, up_y, down_y)
    y_full = placed(
        (4, 2, 4, 192, 384), scalars, y_parts,
        lambda ref, s, half: (
            slice(None), ref[1] if half == 0 else 1 - ref[1], (ref[2] + s) % 4
        ),
    ).reshape(4, 1536, 384)

    def x_slot(ref, s, half):
        from_y = (ref[3] + s) % 4
        quarter = (from_y // 2) * 2 + (ref[1] if half == 0 else 1 - ref[1])
        return slice(None), rows((from_y % 2) * 192, 192), rows(quarter * 384, 384)

    x_full = placed((4, 384, 1536), scalars, x_parts, x_slot)
    own = ordered(scalars, own)
    other = on_chip(own)

    def along_y(value, s, planes):
        return moved(value, lambda x, y, co, z: (x, y + s, co, z) if x in planes else None)

    def given_along_y(parts, planes):
        return [parts[0]] + [along_y(part, s, planes) for s, part in zip(SHIFTS[1:], parts[1:])]

    mixed, right = [], []
    for t in range(3):
        if t > 0:
            own = exchanged(jnp.broadcast_to(piece, (4, 192, 384)), rings(t, True))
            other = on_chip(own)
        theirs, mine, mixed_now, right_now = chain_step(t, scalars, own, other, x_full, y_full)
        mixed.append(mixed_now)
        right.append(right_now)
        total = summed(exchanged(added(mine, on_chip(theirs)), rings(t, False)))

        def hop(x, y, co, z):
            if x == t:
                return x + 1, y, co, z
            if x == 3 - t:
                return x - 1, y, co, z
            return None

        piece = moved(total, hop)
        if t == 0:
            blocks, _ = early_part(along, {0: mixed[0]}, {})
            blocks = ordered(along, given_along_y(blocks, (0, 3)))
            mixed_parts = [blocks] + [
                moved(blocks, lambda x, y, co, z, s=s: (x, y, co, z + s) if x == 0 else None)
                for s in SHIFTS[1:]
            ]

    blocks, right_own = early_part(
        along, {1: mixed[1], 2: mixed[2]}, {1: right[2], 2: right[1], 3: right[0]}
    )
    right_own = given_along_y([right_own] * 4, (1, 2, 3))
    mixed = given_along_y(blocks, (1, 2))

    own = given_along_y([piece] * 4, (0, 3))
    own = ordered(along, own)
    other = on_chip(own)
    late = late_part(along, own, other, y_full, mixed_parts)

    late = exchanged(late, rings(0, False))
    mixed, right_own, late = lax.optimization_barrier((mixed, right_own, late))
    right_own = ordered(along, right_own)
    right_other = on_chip(right_own)
    mixed = ordered(along, mixed)
    grad = grad_part(along, late, mixed, right_own, right_other)
    grad = lax.all_to_all(grad, ("yh", "co", "yl"), 0, 0, tiled=True)
    grad = grad.reshape(2, 2, 2, 192, 384).transpose(3, 1, 0, 2, 4).reshape(1, 192, 8, 384)
    return grad.astype(F32)


def solution(mesh):
    fine = Mesh(mesh.devices.reshape(4, 2, 2, 2, 4), AXES)
    cores = P("x", ("yl", "z"), None, ("yh", "co"))
    env = P(("yl", "z"), ("yh", "co"))

    return jax.shard_map(
        on_device,
        mesh=fine,
        in_specs=(cores, cores, env, env),
        out_specs=cores,
        check_vma=False,
    )
```

```python
import jax
import jax.numpy as jnp
from jax import lax
from jax.experimental import pallas as pl
from jax.experimental.pallas import tpu as pltpu
from jax.sharding import Mesh, PartitionSpec as P


AXES = ("x", "yh", "co", "yl", "z")
BF = jnp.bfloat16
F32 = jnp.float32
VMEM = pl.BlockSpec(memory_space=pltpu.VMEM)
SMEM = pl.BlockSpec(memory_space=pltpu.SMEM)
ANY = pl.BlockSpec(memory_space=pl.ANY)
HBM = pl.BlockSpec(memory_space=pltpu.HBM)
SHIFTS = (0, 1, 3, 2)
LIMIT = pltpu.CompilerParams(vmem_limit_bytes=24 * 2**20)


def index_of(x, y, co, z):
    return (((x * 2 + y // 2) * 2 + co) * 2 + y % 2) * 4 + z


def moved(value, where):
    pairs = []
    for x in range(4):
        for y in range(4):
            for co in range(2):
                for z in range(4):
                    to = where(x, y, co, z)
                    if to is not None:
                        tx, ty, tc, tz = to
                        pairs.append((index_of(x, y, co, z), index_of(tx, ty % 4, tc, tz % 4)))
    return lax.ppermute(value, AXES, pairs)


def on_chip(value, planes=(0, 1, 2, 3)):
    return moved(value, lambda x, y, co, z: (x, y, 1 - co, z) if x in planes else None)


def exchanged(value, groups):
    return lax.all_to_all(value, AXES, 0, 0, axis_index_groups=groups, tiled=True)


def rings(t, left_along_y):
    groups = []
    for x in range(4):
        if t > 0 and x in (0, 3):
            groups += [
                [index_of(x, 2 * h + k, c, other) for c in range(2) for k in range(2)]
                for h in range(2) for other in range(4)
            ]
            continue
        along_y = left_along_y != (x == 3 - t)
        for c in range(2):
            for other in range(4):
                groups.append([
                    index_of(x, k, c, other) if along_y else index_of(x, other, c, k)
                    for k in range(4)
                ])
    return groups


def dot(a, b, dims):
    return lax.dot_general(a, b, (dims, ((), ())), preferred_element_type=F32)


def shape_of(*shape, dtype=BF):
    return jax.ShapeDtypeStruct(shape, dtype)


def rows(start, size):
    return pl.ds(pl.multiple_of(start, size), size)


def put_left(co, own_ref, other_ref, left_s):
    for h, ref in ((co, own_ref), (1 - co, other_ref)):
        for j in range(4):
            left_s[rows(h * 192, 192), j * 384:(j + 1) * 384] = ref[j]


def placed(shape, scalars, pieces, slot):
    def kernel(scalars_ref, *refs):
        out, sems = refs[8:]
        copies = [
            pltpu.make_async_copy(
                refs[2 * n + half], out.at[slot(scalars_ref, s, half)], sems.at[2 * n + half]
            )
            for n, s in enumerate(SHIFTS) for half in range(2)
        ]
        for copy in copies:
            copy.start()
        for copy in copies:
            copy.wait()

    return pl.pallas_call(
        kernel,
        out_shape=shape_of(*shape),
        in_specs=[SMEM] + [ANY] * 8,
        out_specs=VMEM,
        scratch_shapes=[pltpu.SemaphoreType.DMA((8,))],
        compiler_params=LIMIT,
    )(scalars, *pieces)


def summed(parts):
    def kernel(parts_ref, out_ref):
        total = parts_ref[0].astype(F32)
        for n in range(1, 4):
            total += parts_ref[n].astype(F32)
        out_ref[...] = total.astype(BF)

    return pl.pallas_call(
        kernel,
        out_shape=shape_of(192, 384),
        in_specs=[VMEM],
        out_specs=VMEM,
        compiler_params=LIMIT,
    )(parts)


def added(first, second):
    def kernel(first_ref, second_ref, out_ref):
        for n in range(4):
            out_ref[n] = (first_ref[n].astype(F32) + second_ref[n].astype(F32)).astype(BF)

    return pl.pallas_call(
        kernel,
        out_shape=shape_of(4, 192, 384),
        in_specs=[VMEM] * 2,
        out_specs=VMEM,
        compiler_params=LIMIT,
    )(first, second)


def early_part(scalars, mixed, right):
    def kernel(scalars_ref, *refs):
        count = len(mixed) + len(right)
        outs, half_ref, mixed_s, sems = refs[count:count + 4], *refs[count + 4:]
        site, co, y = scalars_ref[0], scalars_ref[1], scalars_ref[3]
        mixed_r = list(zip(mixed, refs[:len(mixed)]))
        right_r = list(zip(right, refs[len(mixed):count]))
        half = rows(co * 768, 768)
        for at, ref in right_r:
            @pl.when(site == at)
            def _():
                copy = pltpu.make_async_copy(ref.at[half], half_ref, sems.at[1])
                copy.start()
                copy.wait()
        for at, ref in mixed_r:
            @pl.when(site == at)
            def _():
                copy = pltpu.make_async_copy(ref, mixed_s, sems.at[0])
                copy.start()
                copy.wait()
                for s, out in zip(SHIFTS, outs):
                    out[...] = mixed_s[(y + s) % 4]

    outs = pl.pallas_call(
        kernel,
        out_shape=(shape_of(384, 384),) * 4 + (shape_of(768, 384),),
        in_specs=[SMEM] + [ANY] * (len(mixed) + len(right)),
        out_specs=(VMEM,) * 5,
        scratch_shapes=[pltpu.VMEM((4, 384, 384), BF), pltpu.SemaphoreType.DMA((2,))],
        compiler_params=LIMIT,
    )(scalars, *mixed.values(), *right.values())
    return outs[:4], outs[4]


def chain_step(t, scalars, own, other, x_full, y_full):
    def kernel(scalars_ref, own_ref, other_ref, x_ref, y_ref,
               theirs_ref, mine_ref, mixed_out, right_out,
               left_s, sum_l, sum_r, mixed_ref, right_ref, sem):
        site, co = scalars_ref[0], scalars_ref[1]
        halves = ((co, mine_ref), (1 - co, theirs_ref))

        @pl.when(site == t)
        def _():
            put_left(co, own_ref, other_ref, left_s)
            for i in range(4):
                mixed_ref[i] = dot(left_s[...], y_ref[i], ((1,), (0,))).astype(BF)
            keep = pltpu.make_async_copy(mixed_ref, mixed_out, sem)
            keep.start()
            sum_l[...] = dot(
                x_ref[...].reshape(1536, 1536), mixed_ref[...].reshape(1536, 384), ((0,), (0,))
            )
            for h, to in halves:
                for j in range(4):
                    to[j] = sum_l[rows(h * 768 + j * 192, 192), :].astype(to.dtype)
            keep.wait()

        @pl.when(site == 3 - t)
        def _():
            for h, ref in ((co, own_ref), (1 - co, other_ref)):
                for j in range(4):
                    right_ref[rows(h * 768 + j * 192, 192), :] = ref[j]
            keep = pltpu.make_async_copy(right_ref, right_out, sem)
            keep.start()
            for i in range(4):
                image = dot(x_ref[i], right_ref[...], ((1,), (0,))).astype(BF)
                part = dot(image, y_ref[i], ((1,), (1,)))
                sum_r[...] = part if i == 0 else sum_r[...] + part
            for h, to in halves:
                for j in range(4):
                    to[j] = sum_r[rows(h * 192, 192), j * 384:(j + 1) * 384].astype(to.dtype)
            keep.wait()

    return pl.pallas_call(
        kernel,
        out_shape=(
            shape_of(4, 192, 384),
            shape_of(4, 192, 384),
            pltpu.HBM((4, 384, 384), BF),
            pltpu.HBM((1536, 384), BF),
        ),
        in_specs=[SMEM] + [VMEM] * 4,
        out_specs=(VMEM, VMEM, HBM, HBM),
        scratch_shapes=[
            pltpu.VMEM((384, 1536), BF),
            pltpu.VMEM((1536, 384), F32),
            pltpu.VMEM((384, 1536), F32),
            pltpu.VMEM((4, 384, 384), BF),
            pltpu.VMEM((1536, 384), BF),
            pltpu.SemaphoreType.DMA,
        ],
        compiler_params=LIMIT,
    )(scalars, own, other, x_full, y_full)


def ordered(scalars, pieces):
    def kernel(scalars_ref, *refs):
        me = jnp.where(scalars_ref[4] == 1, scalars_ref[2], scalars_ref[3])
        for s, ref in zip(SHIFTS, refs[:4]):
            refs[4][(me + 4 - s) % 4] = ref[...]

    return pl.pallas_call(
        kernel,
        out_shape=shape_of(4, *pieces[0].shape),
        in_specs=[SMEM] + [VMEM] * 4,
        out_specs=VMEM,
        compiler_params=LIMIT,
    )(scalars, *pieces)


def late_part(scalars, own, other, y_full, mixed_parts):
    def kernel(scalars_ref, own_ref, other_ref, *refs):
        y_ref, out_ref, env_s, m_s, m_sems = refs[0], *refs[5:]
        site, co, z = scalars_ref[0], scalars_ref[1], scalars_ref[2]
        of_m = [pltpu.make_async_copy(refs[1 + n], m_s.at[n], m_sems.at[n]) for n in range(4)]

        @pl.when(site == 3)
        def _():
            put_left(co, own_ref, other_ref, env_s)
            for i in range(4):
                out_ref[i] = dot(env_s[...], y_ref[i], ((1,), (0,))).astype(BF)

        @pl.when(site == 0)
        def _():
            for copy in of_m:
                copy.start()
            put_left(co, own_ref, other_ref, env_s)
            for n, s in enumerate(SHIFTS):
                of_m[n].wait()
                total = dot(m_s[n, 0], env_s[:, :384], ((1,), (1,)))
                for k in range(1, 4):
                    total += dot(m_s[n, k], env_s[:, k * 384:(k + 1) * 384], ((1,), (1,)))
                out_ref[(z + 4 - s) % 4] = total.astype(BF)

    return pl.pallas_call(
        kernel,
        out_shape=shape_of(4, 384, 384),
        in_specs=[SMEM] + [VMEM] * 3 + [ANY] * 4,
        out_specs=VMEM,
        scratch_shapes=[
            pltpu.VMEM((384, 1536), BF),
            pltpu.VMEM((4, 4, 384, 384), BF),
            pltpu.SemaphoreType.DMA((4,)),
        ],
        compiler_params=LIMIT,
    )(scalars, own, other, y_full, *mixed_parts)


def grad_part(scalars, late, mixed, right, right_other):
    def kernel(scalars_ref, *refs):
        late_r, mixed_r = refs[:2]
        out_ref, mixed_s, right_s, sems = refs[4:]
        site, co = scalars_ref[0], scalars_ref[1]

        def fetched(copies):
            for copy in copies:
                copy.start()
            for copy in copies:
                copy.wait()

        def late_copies():
            return [pltpu.make_async_copy(late_r, mixed_s, sems.at[0])]

        def right_copies(at):
            return [
                pltpu.make_async_copy(refs[at + k], right_s.at[h], sems.at[1 + k])
                for k, h in enumerate((co, 1 - co))
            ]

        @pl.when(site == 0)
        def _():
            fetched(late_copies())
            for q in range(4):
                columns = slice((q // 2) * 192, (q // 2) * 192 + 192)
                block = jnp.concatenate(
                    [mixed_s[2 * (q % 2) + e][:, columns] for e in range(2)], axis=1
                )
                out_ref[2 * q] = block[:192]
                out_ref[2 * q + 1] = block[192:]

        @pl.when(site == 3)
        def _():
            fetched(late_copies() + right_copies(2))

        @pl.when((site == 1) | (site == 2))
        def _():
            fetched([pltpu.make_async_copy(mixed_r, mixed_s, sems.at[0])] + right_copies(2))

        @pl.when(site != 0)
        def _():
            for q in range(4):
                h, r = q // 2, (q % 2) * 384
                total = dot(mixed_s[0], right_s[h, 0, r:r + 384], ((1,), (1,)))
                for k in range(1, 4):
                    total += dot(mixed_s[k], right_s[h, k, r:r + 384], ((1,), (1,)))
                total = total.astype(BF)
                out_ref[2 * q] = total[:192]
                out_ref[2 * q + 1] = total[192:]

    return pl.pallas_call(
        kernel,
        out_shape=shape_of(8, 192, 384),
        in_specs=[SMEM] + [ANY] * 4,
        out_specs=VMEM,
        scratch_shapes=[
            pltpu.VMEM((4, 384, 384), BF),
            pltpu.VMEM((2, 4, 768, 384), BF),
            pltpu.SemaphoreType.DMA((3,)),
        ],
        compiler_params=LIMIT,
    )(scalars, late, mixed, right, right_other)


def on_device(cores_x, cores_y, left_env, right_env):
    site = lax.axis_index("x")
    yh, yl = lax.axis_index("yh"), lax.axis_index("yl")
    co, z = lax.axis_index("co"), lax.axis_index("z")
    y = 2 * yh + yl

    scalars = jnp.stack([site, co, z, y, site // 3]).astype(jnp.int32)
    along = jnp.stack([site, co, z, y, 0]).astype(jnp.int32)

    def half(core, which):
        return jnp.transpose(lax.dynamic_slice_in_dim(core[0], which * 4, 4, axis=1), (1, 0, 2))

    def turned(x, y, co, z):
        return x, (y // 2) * 2 + co, y % 2, z

    def turned_other(x, y, co, z):
        return x, (y // 2) * 2 + co, 1 - y % 2, z

    y_a, y_b = half(cores_y, yl), half(cores_y, 1 - yl)
    x_own, x_out = half(cores_x, co), half(cores_x, 1 - co)
    env = jnp.where(site == 0, left_env, right_env)

    def first_env(s):
        def to(x, y, co, z):
            home = (y // 2) * 2 + co
            if x == 0:
                return x, home + s, y % 2, z
            if x == 3:
                return x, home, y % 2, z + s
            return None

        return to

    own = [moved(env, turned)] + [moved(env, first_env(s)) for s in SHIFTS[1:]]
    y_a, y_b, x_out, own = lax.optimization_barrier((y_a, y_b, x_out, own))
    y_a, y_b = moved(y_a, turned), moved(y_b, turned_other)
    x_other = on_chip(x_out)
    y_a, y_b, x_own, x_other = lax.optimization_barrier((y_a, y_b, x_own, x_other))

    def up_z(x, y, co, z):
        return x, y, co, z + 1

    def down_z(x, y, co, z):
        return x, y, co, z - 1

    def up_y(x, y, co, z):
        return x, y + 1, co, z

    def down_y(x, y, co, z):
        return x, y - 1, co, z

    def spread(first, second, up, down):
        before, after = moved(first, up), moved(second, down)
        first_after, second_before = moved(first, down), moved(second, up)
        across = moved(before, up), moved(after, down)
        return [first, second, first_after, after, before, second_before, *across]

    y_parts = spread(y_a, y_b, up_z, down_z)
    x_parts = spread(x_own, x_other, up_y, down_y)
    y_full = placed(
        (4, 2, 4, 192, 384), scalars, y_parts,
        lambda ref, s, half: (
            slice(None), ref[1] if half == 0 else 1 - ref[1], (ref[2] + s) % 4
        ),
    ).reshape(4, 1536, 384)

    def x_slot(ref, s, half):
        from_y = (ref[3] + s) % 4
        quarter = (from_y // 2) * 2 + (ref[1] if half == 0 else 1 - ref[1])
        return slice(None), rows((from_y % 2) * 192, 192), rows(quarter * 384, 384)

    x_full = placed((4, 384, 1536), scalars, x_parts, x_slot)
    own = ordered(scalars, own)
    other = on_chip(own)

    def along_y(value, s, planes):
        return moved(value, lambda x, y, co, z: (x, y + s, co, z) if x in planes else None)

    def given_along_y(parts, planes):
        return [parts[0]] + [along_y(part, s, planes) for s, part in zip(SHIFTS[1:], parts[1:])]

    mixed, right = [], []
    for t in range(3):
        if t > 0:
            own = exchanged(jnp.broadcast_to(piece, (4, 192, 384)), rings(t, True))
            other = on_chip(own)
        theirs, mine, mixed_now, right_now = chain_step(t, scalars, own, other, x_full, y_full)
        mixed.append(mixed_now)
        right.append(right_now)
        total = summed(exchanged(added(mine, on_chip(theirs)), rings(t, False)))

        def hop(x, y, co, z):
            if x == t:
                return x + 1, y, co, z
            if x == 3 - t:
                return x - 1, y, co, z
            return None

        piece = moved(total, hop)
        if t == 0:
            blocks, _ = early_part(along, {0: mixed[0]}, {})
            blocks = ordered(along, given_along_y(blocks, (0, 3)))
            mixed_parts = [blocks] + [
                moved(blocks, lambda x, y, co, z, s=s: (x, y, co, z + s) if x == 0 else None)
                for s in SHIFTS[1:]
            ]

    blocks, right_own = early_part(
        along, {1: mixed[1], 2: mixed[2]}, {1: right[2], 2: right[1], 3: right[0]}
    )
    right_own = given_along_y([right_own] * 4, (1, 2, 3))
    mixed = given_along_y(blocks, (1, 2))

    own = given_along_y([piece] * 4, (0, 3))
    own = ordered(along, own)
    other = on_chip(own)
    late = late_part(along, own, other, y_full, mixed_parts)

    late = exchanged(late, rings(0, False))
    mixed, right_own, late = lax.optimization_barrier((mixed, right_own, late))
    right_own = ordered(along, right_own)
    right_other = on_chip(right_own)
    mixed = ordered(along, mixed)
    grad = grad_part(along, late, mixed, right_own, right_other)
    grad = lax.all_to_all(grad, ("yh", "co", "yl"), 0, 0, tiled=True)
    grad = grad.reshape(2, 2, 2, 192, 384).transpose(3, 1, 0, 2, 4).reshape(1, 192, 8, 384)
    return grad.astype(F32)


def solution(mesh):
    fine = Mesh(mesh.devices.reshape(4, 2, 2, 2, 4), AXES)
    cores = P("x", ("yl", "z"), None, ("yh", "co"))
    env = P(("yl", "z"), ("yh", "co"))

    return jax.shard_map(
        on_device,
        mesh=fine,
        in_specs=(cores, cores, env, env),
        out_specs=cores,
        check_vma=False,
    )
```
